256 devices in a mesh: ctx: 128 (over z, y_hi, x, core), head: 2 (over y_lo).
Axes of the slice: x: 4, y: 4 (y_hi: 2, y_lo: 2; y = y_hi * 2 + y_lo), z: 8, core: 2. Of those that a mesh axis runs over, the one named last changes fastest.
Arguments:
- query: bfloat16 [16384, 4096], P('ctx', 'head'), may hold values from -80 to 80
- cotangent: bfloat16 [16384, 4096], P('ctx', 'head'), may hold values from -6 to 6
- pool: bfloat16 [256, 128, 2, 4096], P(None, 'ctx', None, 'head'), may hold values from -6 to 6
- block_slot: int32 [256], replicated, may hold values from 0 to 255, each once
- block_length: int32 [256], replicated, may hold values from 1 to 128, as said below
- neighbour_ids: int32 [256, 2], P('ctx'), may hold values from 0 to 255, all different within a row
Outputs:
- attended: bfloat16 [16384, 4096], P('ctx', 'head')
- d_query: bfloat16 [16384, 4096], P('ctx', 'head')
- d_pool: float32 [256, 128, 2, 4096], P(None, 'ctx', None, 'head')
The draws below stay inside these ranges and needn't reach their ends.
Inputs may be any that keep to these rules, and one draw needn't show every extreme that they name: `neighbour_ids`: each group names two different blocks; every block is named by some group. `block_slot`: a permutation of the pool rows. `block_length`: slots past the length are padding; some row is full.
All inputs are finite; a program needn't handle non-finite values.
Results may differ from the reference program's by a relative error of at most 0.005.
Values may be sent and summed in bfloat16 or wider, within the bound.
No kernel may reach another device: no remote copies, remote signals or barrier semaphores. Data moves between devices by JAX's collectives and lax.ppermute only.
A program may use at most 128 MiB of HBM per device.

```python
import math
import jax
import jax.numpy as jnp
from jax import lax

HEADS = 32
HD = 128
GROUP = 64
BTOK = 128
TOKENS = 16384
SEQ = 16384
GROUPS = 256
POOL = 256


def draw_query(key, part):
    values = jax.random.normal(key, (TOKENS, HEADS * HD), jnp.float32)
    return values.astype(jnp.bfloat16)


def draw_block_length(key, part):
    first, second = jax.random.split(jax.random.fold_in(key, 11))
    lengths = jax.random.randint(first, (POOL,), 1, BTOK + 1)
    full_row = jax.random.randint(second, (), 0, POOL)
    return jnp.where(jnp.arange(POOL) == full_row, BTOK, lengths).astype(jnp.int32)


def shard_levels(rng, shape, shards, low, top_value):
    factor_of, own = 1.0, jax.random.fold_in(rng, 6)
    for axis_at, blocks in shards:
        steps = jnp.exp(jax.random.uniform(jax.random.fold_in(own, axis_at), (blocks,), jnp.float32, low / len(shards), top_value / len(shards)))
        factor_of = factor_of * jnp.repeat(steps, shape[axis_at] // blocks).reshape([-1 if axis == axis_at else 1 for axis in range(len(shape))])
    return factor_of


def distinct(key, rows, number_of, top, lift):
    ranking = jax.random.permutation(jax.random.fold_in(key, 1), number_of)
    boost = ranking
    for power in range(3):
        boost = boost * boost // number_of
    boost = boost * lift // number_of
    chance = jax.random.randint(jax.random.fold_in(key, 2), (rows, number_of), 0, 4096) + boost
    holders = jax.random.permutation(jax.random.fold_in(key, 3), rows)[jnp.arange(number_of) % rows]
    chance = jnp.where(jnp.arange(rows)[:, None] == holders[None, :], 1 << 14, chance)
    priority = chance * number_of + jnp.arange(number_of)
    return lax.top_k(priority.astype(jnp.int32), top)[1].astype(jnp.int32)


def gaussian(key, shape, deviation, limit, cuts=(), kind=jnp.bfloat16):
    loudness = shard_levels(key, shape, cuts, -0.22, 0.18) if cuts else 1.0
    values = jax.random.normal(key, shape, jnp.float32) * deviation * loudness
    return jnp.minimum(jnp.maximum(values, -limit), limit).astype(kind)


def setup_inputs(seed: int = 0) -> dict:
    key_list = jax.random.split(jax.random.key(seed), 7)
    return {
        "query": draw_query(jax.random.fold_in(key_list[6], 71), 0),
        "cotangent": gaussian(key_list[1], (TOKENS, HEADS * HD), 1.0, 6.0, ((0, 128), (1, 2))),
        "pool": gaussian(key_list[2], (POOL, BTOK, 2, HEADS * HD), 1.0, 6.0, ((1, 128), (3, 2))),
        "block_slot": jax.random.permutation(key_list[3], POOL).astype(jnp.int32),
        "block_length": draw_block_length(jax.random.fold_in(key_list[6], 71), 0),
        "neighbour_ids": distinct(key_list[5], GROUPS, POOL, 2, 128),
    }


def attend(query_block, grad_block, key_block, value_block, key_mask, live_mask):
    scaling = 1.0 / math.sqrt(HD)
    query_wide = query_block.astype(jnp.float32)
    grad_wide = grad_block.astype(jnp.float32)
    key_wide = key_block.astype(jnp.float32)
    value_wide = value_block.astype(jnp.float32)
    scores = jnp.einsum('bqhd,bkhd->bhqk', query_wide, key_wide) * scaling
    scores = jnp.where(key_mask[:, None, None, :], scores, jnp.float32(-1e+30))
    row_max = lax.optimization_barrier(jnp.max(scores, -1, keepdims=True))
    weights = jnp.exp(scores - row_max)
    probs = weights / lax.optimization_barrier(jnp.sum(weights, -1, keepdims=True))
    probs = probs * live_mask[:, None, :, None].astype(jnp.float32)
    probs_b = probs.astype(jnp.bfloat16)
    result = jnp.einsum('bhqk,bkhd->bqhd', probs_b.astype(jnp.float32), value_wide).astype(jnp.bfloat16)
    dprob = jnp.einsum('bqhd,bkhd->bhqk', grad_wide, value_wide)
    row_delta = lax.optimization_barrier(jnp.sum(probs * dprob, -1, keepdims=True))
    dscore = (probs * (dprob - row_delta) * scaling).astype(jnp.bfloat16)
    dscore_wide = dscore.astype(jnp.float32)
    grad_query = jnp.einsum('bhqk,bkhd->bqhd', dscore_wide, key_wide).astype(jnp.bfloat16)
    grad_key = jnp.einsum('bhqk,bqhd->bkhd', dscore_wide, query_wide)
    grad_value = jnp.einsum('bhqk,bqhd->bkhd', probs_b.astype(jnp.float32), grad_wide)
    return (result, grad_query, grad_key, grad_value)

def row_live(block_index):
    token_pos = block_index[:, None] * GROUP + jnp.arange(GROUP, dtype=jnp.int32)[None, :] - 1
    return (token_pos >= 0) & (jnp.mod(token_pos, SEQ) >= GROUP - 1)

def reference(query, cotangent, pool, block_slot, block_length, neighbour_ids):
    columns = HEADS * HD
    zero_row = jnp.zeros((1, columns), jnp.bfloat16)
    tail_zeros = jnp.zeros((GROUP - 1, columns), jnp.bfloat16)
    shifted = jnp.concatenate([zero_row, query, tail_zeros], 0).reshape(GROUPS + 1, GROUP, HEADS, HD)
    gshift = jnp.concatenate([zero_row, cotangent, tail_zeros], 0).reshape(GROUPS + 1, GROUP, HEADS, HD)
    id_list = jnp.concatenate([neighbour_ids[:1], neighbour_ids], 0).astype(jnp.int32)
    live_list = row_live(jnp.arange(GROUPS + 1, dtype=jnp.int32))

    def group_step(pool_grad, group_item):
        query_block, grad_block, group_ids, live_one = group_item
        pool_rows = block_slot[group_ids].astype(jnp.int32)
        blocks = pool[pool_rows]
        lengths = block_length[pool_rows]
        key_block = blocks[:, :, 0].reshape(1, 2 * BTOK, HEADS, HD)
        value_block = blocks[:, :, 1].reshape(1, 2 * BTOK, HEADS, HD)
        key_mask = (jnp.arange(BTOK)[None, :] < lengths[:, None]).reshape(1, 2 * BTOK)
        result, grad_query, grad_key, grad_value = attend(query_block[None], grad_block[None], key_block, value_block, key_mask, live_one[None])
        update = jnp.stack([grad_key.reshape(2, BTOK, columns), grad_value.reshape(2, BTOK, columns)], 2)
        pool_grad = pool_grad.at[pool_rows].add(update)
        return (pool_grad, (result[0], grad_query[0]))
    start = jnp.zeros(pool.shape, jnp.float32)
    d_pool, (outputs, grads) = lax.scan(group_step, start, (shifted, gshift, id_list, live_list))
    attended = outputs.reshape((GROUPS + 1) * GROUP, columns)[1:TOKENS + 1]
    d_query = grads.reshape((GROUPS + 1) * GROUP, columns)[1:TOKENS + 1]
    return (attended, d_query, d_pool)
```

```python
import functools
import math

import jax
import jax.numpy as jnp
from jax import lax
from jax.experimental import pallas as pl
from jax.experimental.pallas import tpu as pltpu
from jax.sharding import PartitionSpec as P

HD = 128
GROUP = 64
BTOK = 128
POOL = 256
CTX = 128
LINE = 16
PLANE = 8
USES = 4
BF = jnp.bfloat16
F32 = jnp.float32


def ctx_of(s, m):
    return (s // 2) * 16 + m * 2 + s % 2


LINES = [[ctx_of(s, m) for s in range(LINE)] for m in range(PLANE)]
PLANES = [[ctx_of(s, m) for m in range(PLANE)] for s in range(LINE)]
ORDER = [(0, 0), (0, 1)] + [(dz, dc) for dz in (4, 3, 5, 2, 6, 1, 7) for dc in (0, 1)]


def moved(s, dz, dc):
    return ((s // 2 + dz) % 8) * 2 + (s % 2 + dc) % 2


def line_move(value, dz, dc):
    pairs = [(ctx_of(s, m), ctx_of(moved(s, dz, dc), m)) for s in range(LINE) for m in range(PLANE)]
    return lax.ppermute(value, "ctx", pairs)


def ring_move(value, step):
    return lax.ppermute(value, "ctx", [(i, (i + step) % CTX) for i in range(CTX)])


def exchange(value, groups):
    return lax.all_to_all(
        value, "ctx", split_axis=0, concat_axis=0, tiled=True, axis_index_groups=groups
    )


def use_row(ids_ref, slot_ref, ctx, u):
    k = lax.rem(ctx * USES + u + 2 * POOL - 2, 2 * POOL)
    return slot_ref[ids_ref[k]]


def split_rows(q_ref, g_ref, prev_ref, meta_ref, out_ref):
    rows = lax.broadcasted_iota(jnp.int32, (2 * GROUP, HD), 0)
    s = meta_ref[0]
    for k, (dz, dc) in enumerate(ORDER):
        head = moved(s, dz, dc)
        cols = pl.ds(pl.multiple_of(head * HD, HD), HD)
        for n, ref in enumerate((q_ref, g_ref)):
            wide = pltpu.roll(ref[:, cols].astype(F32), 1, 0)
            first = prev_ref[n : n + 1, cols].astype(F32)
            out_ref[k, n] = jnp.where(rows == 0, first, wide).astype(BF)


def join_rows(x_ref, meta_ref, att_ref, dq_ref, edge_ref):
    s = meta_ref[0]
    for k, (dz, dc) in enumerate(ORDER):
        head = moved(s, dz, dc)
        cols = pl.ds(pl.multiple_of(head * HD, HD), HD)
        for n, ref in enumerate((att_ref, dq_ref)):
            wide = x_ref[k, n].astype(F32)
            ref[:, cols] = pltpu.roll(wide, 2 * GROUP - 1, 0).astype(BF)
            edge_ref[n : n + 1, cols] = wide[0:1].astype(BF)


def close_rows(att_in, dq_in, edge_ref, att_ref, dq_ref):
    rows = lax.broadcasted_iota(jnp.int32, att_in.shape, 0)
    last = rows == 2 * GROUP - 1
    for n, (ref, out) in enumerate(((att_in, att_ref), (dq_in, dq_ref))):
        edge = edge_ref[n : n + 1, :].astype(F32)
        out[...] = jnp.where(last, edge, ref[...].astype(F32)).astype(BF)


def pick(ids_ref, slot_ref, x_ref, out_ref, wide_ref):
    m = pl.program_id(0)

    @pl.when(m == 0)
    def _():
        for s in range(LINE):
            for n in range(2):
                wide_ref[pl.ds((n * LINE + s) * POOL, POOL), :] = x_ref[s, n].astype(F32)

    @pl.loop(0, LINE)
    def _(s):
        ctx = (s // 2) * 16 + m * 2 + s % 2
        for u in range(USES):
            row = use_row(ids_ref, slot_ref, ctx, u)
            for n in range(2):
                tile = wide_ref[pl.ds(n * LINE * POOL + row, LINE, stride=POOL), :]
                out_ref[0, s * USES + u, n] = tile.astype(BF)


def attend(ids_ref, slot_ref, len_ref, meta_ref, qg_ref, kv_ref, out_ref, grad_ref):
    scaling = 1.0 / math.sqrt(HD)
    s, m = meta_ref[2 + pl.program_id(0)], meta_ref[1]
    ctx = (s // 2) * 16 + m * 2 + s % 2
    place = lax.broadcasted_iota(jnp.int32, (1, 2 * BTOK), 1)
    within = place % BTOK
    slot = ((within % LINE) // 2) * 16 + (within // LINE) * 2 + within % 2
    row_at = lax.broadcasted_iota(jnp.int32, (GROUP, 1), 0)
    nt = (((1,), (1,)), ((), ()))
    tn = (((0,), (0,)), ((), ()))
    dot = functools.partial(lax.dot_general, preferred_element_type=F32)
    nn = (((1,), (0,)), ((), ()))
    for group in range(2):
        query = qg_ref[0, 0, group * GROUP : (group + 1) * GROUP, :]
        grad = qg_ref[0, 1, group * GROUP : (group + 1) * GROUP, :]
        lens = [len_ref[use_row(ids_ref, slot_ref, ctx, 2 * group + n)] for n in range(2)]
        mask = slot < jnp.where(place < BTOK, lens[0], lens[1])
        keys, values = (
            jnp.concatenate(
                [kv_ref[:, 2 * group + n, w].reshape(BTOK, HD) for n in range(2)], 0
            )
            for w in range(2)
        )
        scores = dot(query, keys, nt) * scaling
        scores = jnp.where(mask, scores, F32(-1e30))
        weights = jnp.exp(scores - jnp.max(scores, -1, keepdims=True))
        probs = weights / jnp.sum(weights, -1, keepdims=True)
        if group == 0:
            probs = jnp.where((row_at == 0) | (ctx > 0), probs, F32(0))
        probs_b = probs.astype(BF)
        result = dot(probs_b, values, nn)
        dprob = dot(grad, values, nt)
        delta = jnp.sum(probs * dprob, -1, keepdims=True)
        dscore = (probs * (dprob - delta) * scaling).astype(BF)
        grad_query = dot(dscore, keys, nn)
        grad_key = dot(dscore, query, tn).astype(BF)
        grad_value = dot(probs_b, grad, tn).astype(BF)
        out_ref[0, 0, group * GROUP : (group + 1) * GROUP, :] = result.astype(BF)
        out_ref[0, 1, group * GROUP : (group + 1) * GROUP, :] = grad_query.astype(BF)
        for n in range(2):
            part = slice(n * BTOK, (n + 1) * BTOK)
            grad_ref[:, 2 * group + n, 0] = grad_key[part].reshape(PLANE, LINE, HD)
            grad_ref[:, 2 * group + n, 1] = grad_value[part].reshape(PLANE, LINE, HD)


def gather_grads(ids_ref, slot_ref, x_ref, out_ref, sum_ref):
    m = pl.program_id(0)

    @pl.when(m == 0)
    def _():
        sum_ref[...] = jnp.zeros_like(sum_ref)

    @pl.loop(0, LINE)
    def _(s):
        ctx = (s // 2) * 16 + m * 2 + s % 2
        for u in range(USES):
            row = use_row(ids_ref, slot_ref, ctx, u)
            at = pl.ds(pl.multiple_of(row * 2 * LINE, 2 * LINE), 2 * LINE)
            sum_ref[at, :] += x_ref[0, s * USES + u].reshape(2 * LINE, HD).astype(F32)

    @pl.when(m == PLANE - 1)
    def _():
        for s in range(LINE):
            for n in range(2):
                out_ref[s, n] = sum_ref[pl.ds(n * LINE + s, POOL, stride=2 * LINE), :].astype(BF)


VMEM = pl.BlockSpec(memory_space=pltpu.VMEM)
SMEM = pl.BlockSpec(memory_space=pltpu.SMEM)
LIMIT = pltpu.CompilerParams(vmem_limit_bytes=40 << 20)


def shape(*dims, dtype=BF):
    return jax.ShapeDtypeStruct(dims, dtype)


def per_device(query, cotangent, pool, block_slot, block_length, neighbour_ids):
    columns = query.shape[1]
    rows = query.shape[0]
    me = lax.axis_index("ctx")
    s = (me // 16) * 2 + me % 2
    m = (me // 2) % 8
    meta = jnp.stack([s, m] + [moved(s, -dz, -dc) for dz, dc in ORDER]).astype(jnp.int32)

    sent = pool.reshape(POOL, 2, LINE, HD).transpose(2, 1, 0, 3)
    line_kv = exchange(sent, LINES)

    own = lax.dynamic_update_slice(
        jnp.zeros((CTX * USES,), jnp.int32), neighbour_ids.reshape(-1), (me * USES,)
    )
    ids = lax.psum(own, "ctx")

    edge = jnp.stack([query[rows - 1], cotangent[rows - 1]])
    before = ring_move(edge, 1)
    split = pl.pallas_call(
        split_rows,
        out_shape=shape(LINE, 2, rows, HD),
        in_specs=[VMEM, VMEM, VMEM, SMEM],
        out_specs=VMEM,
        compiler_params=LIMIT,
    )(query, cotangent, before, meta)

    picked = pl.pallas_call(
        pick,
        out_shape=shape(PLANE, LINE * USES, 2, LINE, HD),
        grid_spec=pltpu.PrefetchScalarGridSpec(
            num_scalar_prefetch=2,
            grid=(PLANE,),
            in_specs=[pl.BlockSpec((LINE, 2, POOL, HD), lambda i, *_: (0, 0, 0, 0))],
            out_specs=pl.BlockSpec((1, LINE * USES, 2, LINE, HD), lambda i, *_: (i, 0, 0, 0, 0)),
            scratch_shapes=[pltpu.VMEM((2 * LINE * POOL, HD), F32)],
        ),
        compiler_params=LIMIT,
    )(ids, block_slot, line_kv)
    fetched = exchange(picked, PLANES)

    moved_rows = [split[0]] + [
        line_move(split[k], *ORDER[k]) for k in range(1, LINE)
    ]
    head_rows = jnp.stack(moved_rows)

    results, grads = pl.pallas_call(
        attend,
        out_shape=(shape(LINE, 2, rows, HD), shape(PLANE, LINE * USES, 2, LINE, HD)),
        grid_spec=pltpu.PrefetchScalarGridSpec(
            num_scalar_prefetch=4,
            grid=(LINE,),
            in_specs=[
                pl.BlockSpec((1, 2, rows, HD), lambda i, *_: (i, 0, 0, 0)),
                pl.BlockSpec(
                    (PLANE, USES, 2, LINE, HD), lambda i, a, b, c, t: (0, t[2 + i], 0, 0, 0)
                ),
            ],
            out_specs=(
                pl.BlockSpec((1, 2, rows, HD), lambda i, *_: (i, 0, 0, 0)),
                pl.BlockSpec(
                    (PLANE, USES, 2, LINE, HD), lambda i, a, b, c, t: (0, t[2 + i], 0, 0, 0)
                ),
            ),
        ),
        compiler_params=LIMIT,
    )(ids, block_slot, block_length, meta, head_rows, fetched)

    returned = exchange(grads, PLANES)

    back = [results[0]] + [
        line_move(results[k], -ORDER[k][0], -ORDER[k][1]) for k in range(1, LINE)
    ]
    att_part, dq_part, edge_out = pl.pallas_call(
        join_rows,
        out_shape=(shape(rows, columns), shape(rows, columns), shape(2, columns)),
        in_specs=[VMEM, SMEM],
        out_specs=(VMEM, VMEM, VMEM),
        compiler_params=LIMIT,
    )(jnp.stack(back), meta)
    after = ring_move(edge_out, -1)
    attended, d_query = pl.pallas_call(
        close_rows,
        out_shape=(shape(rows, columns), shape(rows, columns)),
        in_specs=[VMEM, VMEM, VMEM],
        out_specs=(VMEM, VMEM),
        compiler_params=LIMIT,
    )(att_part, dq_part, after)

    summed = pl.pallas_call(
        gather_grads,
        out_shape=shape(LINE, 2, POOL, HD),
        grid_spec=pltpu.PrefetchScalarGridSpec(
            num_scalar_prefetch=2,
            grid=(PLANE,),
            in_specs=[pl.BlockSpec((1, LINE * USES, 2, LINE, HD), lambda i, *_: (i, 0, 0, 0, 0))],
            out_specs=pl.BlockSpec((LINE, 2, POOL, HD), lambda i, *_: (0, 0, 0, 0)),
            scratch_shapes=[pltpu.VMEM((POOL * 2 * LINE, HD), F32)],
        ),
        compiler_params=LIMIT,
    )(ids, block_slot, returned)
    own_grads = exchange(summed, LINES)
    d_pool = own_grads.transpose(2, 1, 0, 3).reshape(pool.shape).astype(F32)
    return (attended, d_query, d_pool)


def solution(mesh):
    placed = (
        P("ctx", "head"),
        P("ctx", "head"),
        P(None, "ctx", None, "head"),
        P(),
        P(),
        P("ctx", None),
    )
    return jax.shard_map(
        per_device,
        mesh=mesh,
        in_specs=placed,
        out_specs=(P("ctx", "head"), P("ctx", "head"), P(None, "ctx", None, "head")),
        check_vma=False,
    )
```

```python
import functools
import math

import jax
import jax.numpy as jnp
from jax import lax
from jax.experimental import pallas as pl
from jax.experimental.pallas import tpu as pltpu
from jax.sharding import PartitionSpec as P

HD = 128
GROUP = 64
BTOK = 128
POOL = 256
CTX = 128
LINE = 16
PLANE = 8
USES = 4
BF = jnp.bfloat16
F32 = jnp.float32


def ctx_of(s, m):
    return (s // 2) * 16 + m * 2 + s % 2


LINES = [[ctx_of(s, m) for s in range(LINE)] for m in range(PLANE)]
PLANES = [[ctx_of(s, m) for m in range(PLANE)] for s in range(LINE)]
STEPS = (0, 4, 3, 5, 2, 6, 1, 7)


def line_move(value, dz, dc):
    pairs = [
        (ctx_of(s, m), ctx_of((s // 2 + dz) % 8 * 2 + (s % 2 + dc) % 2, m))
        for s in range(LINE)
        for m in range(PLANE)
    ]
    return lax.ppermute(value, "ctx", pairs)


def ring_move(value, step):
    return lax.ppermute(value, "ctx", [(i, (i + step) % CTX) for i in range(CTX)])


def exchange(value, groups):
    return lax.all_to_all(
        value, "ctx", split_axis=0, concat_axis=0, tiled=True, axis_index_groups=groups
    )


def use_row(rows_ref, ctx, u):
    return rows_ref[(ctx * USES + u - 2) & (2 * POOL - 1)]


def head_columns(meta_ref, dz, dc):
    head = ((meta_ref[0] >> 1) + dz & 7) * 2 + (meta_ref[0] + dc & 1)
    return pl.ds(pl.multiple_of(head * HD, HD), HD)


def late_rows(ref, prev_ref, n, cols):
    rows = lax.broadcasted_iota(jnp.int32, (2 * GROUP, HD), 0)
    wide = pltpu.roll(ref[:, cols].astype(F32), 1, 0)
    return jnp.where(rows == 0, prev_ref[n : n + 1, cols].astype(F32), wide).astype(BF)


def split_other(q_ref, g_ref, prev_ref, meta_ref, out_ref):
    for k, dz in enumerate(STEPS):
        cols = head_columns(meta_ref, dz, 1)
        for n, ref in enumerate((q_ref, g_ref)):
            out_ref[k, n] = late_rows(ref, prev_ref, n, cols)


def split_own(q_ref, g_ref, prev_ref, meta_ref, other_ref, *out_refs):
    for k, dz in enumerate(STEPS):
        cols = head_columns(meta_ref, dz, 0)
        for n, ref in enumerate((q_ref, g_ref)):
            out_refs[k][0, n] = late_rows(ref, prev_ref, n, cols)
        out_refs[k][1] = other_ref[k]


def join_rows(*refs):
    own_refs, (other_ref, meta_ref, att_ref, dq_ref, edge_ref) = refs[:8], refs[8:]
    for k, dz in enumerate(STEPS):
        for dc in range(2):
            cols = head_columns(meta_ref, dz, dc)
            for n, ref in enumerate((att_ref, dq_ref)):
                wide = (other_ref[k, n] if dc else own_refs[k][0, n]).astype(F32)
                ref[:, cols] = pltpu.roll(wide, 2 * GROUP - 1, 0).astype(BF)
                edge_ref[n : n + 1, cols] = wide[0:1].astype(BF)


def close_rows(att_in, dq_in, edge_ref, att_ref, dq_ref):
    rows = lax.broadcasted_iota(jnp.int32, att_in.shape, 0)
    last = rows == 2 * GROUP - 1
    for n, (ref, out) in enumerate(((att_in, att_ref), (dq_in, dq_ref))):
        edge = edge_ref[n : n + 1, :].astype(F32)
        out[...] = jnp.where(last, edge, ref[...].astype(F32)).astype(BF)


def pick(rows_ref, x_ref, out_ref, wide_ref, block_ref):
    m = pl.program_id(0)

    @pl.when(m == 0)
    def _():
        for s in range(LINE):
            wide_ref[pl.ds(s, 2 * POOL, stride=LINE), :] = x_ref[s].astype(F32)

        @pl.loop(0, POOL // 8)
        def _(i):
            at = pl.ds(pl.multiple_of(i * 256, 256), 256)
            block_ref[pl.ds(i * 8, 8)] = wide_ref[at, :].astype(BF).reshape(8, 2, LINE, HD)

    @pl.loop(0, LINE, unroll=4)
    def _(s):
        ctx = (s >> 1) * 16 + m * 2 + (s & 1)
        for u in range(USES):
            out_ref[0, s * USES + u] = block_ref[use_row(rows_ref, ctx, u)]


def attend(rows_ref, len_ref, meta_ref, qg_ref, kv_ref, out_ref, grad_ref):
    scaling = 1.0 / math.sqrt(HD)
    m = meta_ref[1]
    place = lax.broadcasted_iota(jnp.int32, (1, 2 * BTOK), 1)
    within = place % BTOK
    slot = ((within % LINE) // 2) * 16 + (within // LINE) * 2 + within % 2
    row_at = lax.broadcasted_iota(jnp.int32, (GROUP, 1), 0)
    nn, nt, tn = (((((i,), (j,)), ((), ()))) for i, j in ((1, 0), (1, 1), (0, 0)))
    dot = functools.partial(lax.dot_general, preferred_element_type=F32)
    work = []
    for device in range(2):
        s = meta_ref[2 + 2 * pl.program_id(0) + device]
        ctx = (s >> 1) * 16 + m * 2 + (s & 1)
        for group in range(2):
            lens = [len_ref[use_row(rows_ref, ctx, 2 * group + n)] for n in range(2)]
            mask = slot < jnp.where(place < BTOK, lens[0], lens[1])
            rows = slice(group * GROUP, (group + 1) * GROUP)
            at = (s & 1) * USES + 2 * group
            keys, values = (
                jnp.concatenate([kv_ref[:, at + n, w].reshape(BTOK, HD) for n in range(2)], 0)
                for w in range(2)
            )
            query, grad = qg_ref[device, 0, rows, :], qg_ref[device, 1, rows, :]
            work.append((device, group, rows, at, ctx, mask, query, grad, keys, values))
    scored = [dot(query, keys, nt) for *_, query, _, keys, _ in work]
    dprobs = [dot(grad, values, nt) for *_, grad, _, values in work]
    soft = []
    for item, scores, dprob in zip(work, scored, dprobs):
        group, ctx, mask = item[1], item[4], item[5]
        scores = jnp.where(mask, scores * scaling, F32(-1e30))
        weights = jnp.exp(scores - jnp.max(scores, -1, keepdims=True))
        probs = weights * (1.0 / jnp.sum(weights, -1, keepdims=True))
        if group == 0:
            probs = jnp.where((row_at == 0) | (ctx > 0), probs, F32(0))
        delta = jnp.sum(probs * dprob, -1, keepdims=True)
        soft.append((probs.astype(BF), (probs * (dprob - delta) * scaling).astype(BF)))
    for (device, _, rows, _, _, _, _, _, keys, values), (probs_b, dscore) in zip(work, soft):
        out_ref[device, 0, rows, :] = dot(probs_b, values, nn).astype(BF)
        out_ref[device, 1, rows, :] = dot(dscore, keys, nn).astype(BF)
    for (_, _, _, at, _, _, query, grad, _, _), (probs_b, dscore) in zip(work, soft):
        grad_key = dot(dscore, query, tn).astype(BF)
        grad_value = dot(probs_b, grad, tn).astype(BF)
        for n in range(2):
            part = slice(n * BTOK, (n + 1) * BTOK)
            grad_ref[:, at + n, 0] = grad_key[part].reshape(PLANE, LINE, HD)
            grad_ref[:, at + n, 1] = grad_value[part].reshape(PLANE, LINE, HD)


def gather_grads(rows_ref, x_ref, out_ref, *sum_refs):
    m = pl.program_id(0)

    @pl.when(m == 0)
    def _():
        for ref in sum_refs:
            ref[...] = jnp.zeros_like(ref)

    @pl.loop(0, LINE, unroll=4)
    def _(s):
        ctx = (s >> 1) * 16 + m * 2 + (s & 1)
        for u in range(USES):
            row = use_row(rows_ref, ctx, u)
            at = pl.ds(pl.multiple_of(row * 8, 8), 8)
            for n in range(2):
                wide = x_ref[0, s * USES + u, n].astype(F32)
                for half in range(2):
                    sum_refs[2 * n + half][at, :] += wide[8 * half : 8 * half + 8]

    @pl.when(m == PLANE - 1)
    def _():
        for s in range(LINE):
            for n in range(2):
                part = sum_refs[2 * n + s // 8][pl.ds(s % 8, POOL, stride=8), :]
                out_ref[s, n] = part.astype(BF)


def spread(x_ref, out_ref):
    for head in range(LINE):
        for n in range(2):
            part = x_ref[head, n].astype(F32)
            out_ref[pl.ds(2 * head + n, part.shape[0], stride=2 * LINE), :] = part


VMEM = pl.BlockSpec(memory_space=pltpu.VMEM)
SMEM = pl.BlockSpec(memory_space=pltpu.SMEM)
LIMIT = pltpu.CompilerParams(vmem_limit_bytes=40 << 20)
LARGE = pltpu.CompilerParams(vmem_limit_bytes=60 << 20)


def shape(*dims, dtype=BF):
    return jax.ShapeDtypeStruct(dims, dtype)


def per_device(query, cotangent, pool, block_slot, block_length, neighbour_ids):
    columns = query.shape[1]
    rows = query.shape[0]
    me = lax.axis_index("ctx")
    z, core = me // 16, me % 2
    members = [(z - dz) % 8 * 2 + (core + dc) % 2 for dz in STEPS for dc in range(2)]
    meta = jnp.stack([z * 2 + core, (me // 2) % 8] + members).astype(jnp.int32)

    sent = pool.reshape(POOL, 2, LINE, HD).transpose(2, 0, 1, 3).reshape(LINE, 2 * POOL, HD)
    line_kv = exchange(sent, LINES)

    own = lax.dynamic_update_slice(
        jnp.zeros((CTX * USES,), jnp.int32), block_slot[neighbour_ids.reshape(-1)], (me * USES,)
    )
    pool_rows = lax.psum(own, "ctx")

    before = ring_move(jnp.stack([query[rows - 1], cotangent[rows - 1]]), 1)
    pool_rows, before = lax.optimization_barrier((pool_rows, before))
    other = pl.pallas_call(
        split_other,
        out_shape=shape(8, 2, rows, HD),
        in_specs=[VMEM, VMEM, VMEM, SMEM],
        out_specs=VMEM,
        compiler_params=LIMIT,
    )(query, cotangent, before, meta)
    split = pl.pallas_call(
        split_own,
        out_shape=[shape(2, 2, rows, HD)] * 8,
        in_specs=[VMEM, VMEM, VMEM, SMEM, VMEM],
        out_specs=[VMEM] * 8,
        compiler_params=LIMIT,
    )(query, cotangent, before, meta, line_move(other, 0, 1))

    plane_spec = pl.BlockSpec((1, LINE * USES, 2, LINE, HD), lambda i, *_: (i, 0, 0, 0, 0))
    line_spec = pl.BlockSpec((LINE, 2, POOL, HD), lambda i, *_: (0, 0, 0, 0))
    picked = pl.pallas_call(
        pick,
        out_shape=shape(PLANE, LINE * USES, 2, LINE, HD),
        grid_spec=pltpu.PrefetchScalarGridSpec(
            num_scalar_prefetch=1,
            grid=(PLANE,),
            in_specs=[pl.BlockSpec((LINE, 2 * POOL, HD), lambda i, *_: (0, 0, 0))],
            out_specs=plane_spec,
            scratch_shapes=[
                pltpu.VMEM((2 * LINE * POOL, HD), F32),
                pltpu.VMEM((POOL, 2, LINE, HD), BF),
            ],
        ),
        compiler_params=LARGE,
        cost_estimate=pl.CostEstimate(flops=0, transcendentals=0, bytes_accessed=24 << 20),
    )(pool_rows, line_kv)
    picked, split = lax.optimization_barrier((picked, split))
    fetched = exchange(picked, PLANES)

    head_rows = jnp.concatenate(
        [split[0]] + [line_move(split[k], STEPS[k], 0) for k in range(1, 8)]
    )

    rows_spec = pl.BlockSpec((2, 2, rows, HD), lambda i, *_: (i, 0, 0, 0))
    uses_spec = pl.BlockSpec(
        (PLANE, 2 * USES, 2, LINE, HD), lambda i, r, n, meta: (0, meta[2 + 2 * i] >> 1, 0, 0, 0)
    )
    results, grads = pl.pallas_call(
        attend,
        out_shape=(shape(LINE, 2, rows, HD), shape(PLANE, LINE * USES, 2, LINE, HD)),
        grid_spec=pltpu.PrefetchScalarGridSpec(
            num_scalar_prefetch=3,
            grid=(LINE // 2,),
            in_specs=[rows_spec, uses_spec],
            out_specs=(rows_spec, uses_spec),
        ),
        compiler_params=LARGE,
    )(pool_rows, block_length, meta, head_rows, fetched)

    returned = exchange(grads, PLANES)

    results = results.reshape(8, 2, 2, rows, HD)
    back = [results[0]] + [line_move(results[k], -STEPS[k], 0) for k in range(1, 8)]
    att_part, dq_part, edge_out = pl.pallas_call(
        join_rows,
        out_shape=(shape(rows, columns), shape(rows, columns), shape(2, columns)),
        in_specs=[VMEM] * 9 + [SMEM],
        out_specs=(VMEM, VMEM, VMEM),
        compiler_params=LIMIT,
    )(*back, line_move(jnp.stack([part[1] for part in back]), 0, 1), meta)
    returned, edge_out = lax.optimization_barrier((returned, edge_out))
    summed = pl.pallas_call(
        gather_grads,
        out_shape=shape(LINE, 2, POOL, HD),
        grid_spec=pltpu.PrefetchScalarGridSpec(
            num_scalar_prefetch=1,
            grid=(PLANE,),
            in_specs=[plane_spec],
            out_specs=line_spec,
            scratch_shapes=[pltpu.VMEM((POOL * 8, HD), F32)] * 4,
        ),
        compiler_params=LIMIT,
    )(pool_rows, returned)
    after = ring_move(edge_out, -1)
    attended, d_query = pl.pallas_call(
        close_rows,
        out_shape=(shape(rows, columns), shape(rows, columns)),
        in_specs=[VMEM, VMEM, VMEM],
        out_specs=(VMEM, VMEM),
        compiler_params=LIMIT,
    )(att_part, dq_part, after)

    own_grads = exchange(summed, LINES)
    chunk = 32
    wide = pl.pallas_call(
        spread,
        out_shape=shape(POOL * 2 * LINE, HD, dtype=F32),
        grid=(POOL // chunk,),
        in_specs=[pl.BlockSpec((LINE, 2, chunk, HD), lambda i: (0, 0, i, 0))],
        out_specs=pl.BlockSpec((chunk * 2 * LINE, HD), lambda i: (i, 0)),
        compiler_params=LIMIT,
    )(own_grads)
    d_pool = wide.reshape(POOL, LINE, 2, HD).transpose(0, 2, 1, 3).reshape(pool.shape)
    return (attended, d_query, d_pool)


def solution(mesh):
    placed = (
        P("ctx", "head"),
        P("ctx", "head"),
        P(None, "ctx", None, "head"),
        P(),
        P(),
        P("ctx", None),
    )
    return jax.shard_map(
        per_device,
        mesh=mesh,
        in_specs=placed,
        out_specs=(P("ctx", "head"), P("ctx", "head"), P(None, "ctx", None, "head")),
        check_vma=False,
    )
```

```python
import functools
import math

import jax
import jax.numpy as jnp
from jax import lax
from jax.experimental import pallas as pl
from jax.experimental.pallas import tpu as pltpu
from jax.sharding import PartitionSpec as P

HD = 128
GROUP = 64
BTOK = 128
POOL = 256
CTX = 128
LINE = 16
PLANE = 8
USES = 4
BF = jnp.bfloat16
F32 = jnp.float32


def ctx_of(s, m):
    return (s // 2) * 16 + m * 2 + s % 2


LINES = [[ctx_of(s, m) for s in range(LINE)] for m in range(PLANE)]
PLANES = [[ctx_of(s, m) for m in range(PLANE)] for s in range(LINE)]
STEPS = (0, 4, 3, 5, 2, 6, 1, 7)


def line_move(value, dz, dc):
    pairs = [
        (ctx_of(s, m), ctx_of((s // 2 + dz) % 8 * 2 + (s % 2 + dc) % 2, m))
        for s in range(LINE)
        for m in range(PLANE)
    ]
    return lax.ppermute(value, "ctx", pairs)


def ring_move(value, step):
    return lax.ppermute(value, "ctx", [(i, (i + step) % CTX) for i in range(CTX)])


def exchange(value, groups):
    return lax.all_to_all(
        value, "ctx", split_axis=0, concat_axis=0, tiled=True, axis_index_groups=groups
    )


def use_row(rows_ref, ctx, u):
    return rows_ref[(ctx * USES + u - 2) & (2 * POOL - 1)]


def head_columns(meta_ref, dz, dc):
    head = ((meta_ref[0] >> 1) + dz & 7) * 2 + (meta_ref[0] + dc & 1)
    return pl.ds(pl.multiple_of(head * HD, HD), HD)


def late_rows(ref, prev_ref, n, cols):
    rows = lax.broadcasted_iota(jnp.int32, (2 * GROUP, HD), 0)
    wide = pltpu.roll(ref[:, cols].astype(F32), 1, 0)
    return jnp.where(rows == 0, prev_ref[n : n + 1, cols].astype(F32), wide).astype(BF)


def split_other(q_ref, g_ref, prev_ref, meta_ref, out_ref):
    for k, dz in enumerate(STEPS):
        cols = head_columns(meta_ref, dz, 1)
        for n, ref in enumerate((q_ref, g_ref)):
            out_ref[k, n] = late_rows(ref, prev_ref, n, cols)


def split_own(q_ref, g_ref, prev_ref, meta_ref, other_ref, *out_refs):
    for k, dz in enumerate(STEPS):
        cols = head_columns(meta_ref, dz, 0)
        for n, ref in enumerate((q_ref, g_ref)):
            out_refs[k][0, n] = late_rows(ref, prev_ref, n, cols)
        out_refs[k][1] = other_ref[k]


def join_rows(*refs):
    own_refs, (other_ref, meta_ref, att_ref, dq_ref, edge_ref) = refs[:8], refs[8:]
    for k, dz in enumerate(STEPS):
        for dc in range(2):
            cols = head_columns(meta_ref, dz, dc)
            for n, ref in enumerate((att_ref, dq_ref)):
                wide = (other_ref[k, n] if dc else own_refs[k][0, n]).astype(F32)
                ref[:, cols] = pltpu.roll(wide, 2 * GROUP - 1, 0).astype(BF)
                edge_ref[n : n + 1, cols] = wide[0:1].astype(BF)


def close_rows(att_in, dq_in, edge_ref, att_ref, dq_ref):
    rows = lax.broadcasted_iota(jnp.int32, att_in.shape, 0)
    last = rows == 2 * GROUP - 1
    for n, (ref, out) in enumerate(((att_in, att_ref), (dq_in, dq_ref))):
        edge = edge_ref[n : n + 1, :].astype(F32)
        out[...] = jnp.where(last, edge, ref[...].astype(F32)).astype(BF)


def pick(rows_ref, x_ref, out_ref, wide_ref, block_ref):
    m = pl.program_id(0)

    @pl.when(m == 0)
    def _():
        for s in range(LINE):
            wide_ref[pl.ds(s, 2 * POOL, stride=LINE), :] = x_ref[s].astype(F32)

        @pl.loop(0, POOL // 8)
        def _(i):
            at = pl.ds(pl.multiple_of(i * 256, 256), 256)
            block_ref[pl.ds(i * 8, 8)] = wide_ref[at, :].astype(BF).reshape(8, 2, LINE, HD)

    for near in range(2):

        @pl.loop(0, LINE, unroll=4)
        def _(s):
            ctx = (s >> 1) * 16 + (2 * m + near) * 2 + (s & 1)
            for u in range(USES):
                out_ref[near, s * USES + u] = block_ref[use_row(rows_ref, ctx, u)]


def attend(rows_ref, len_ref, meta_ref, qg_ref, kv_ref, out_ref, grad_ref):
    scaling = 1.0 / math.sqrt(HD)
    m = meta_ref[1]
    place = lax.broadcasted_iota(jnp.int32, (1, 2 * BTOK), 1)
    within = place % BTOK
    slot = ((within % LINE) // 2) * 16 + (within // LINE) * 2 + within % 2
    row_at = lax.broadcasted_iota(jnp.int32, (GROUP, 1), 0)
    nn, nt, tn = (((((i,), (j,)), ((), ()))) for i, j in ((1, 0), (1, 1), (0, 0)))
    dot = functools.partial(lax.dot_general, preferred_element_type=F32)
    work = []
    for chip, dc in ((0, 0), (0, 1), (1, 0), (1, 1)):
        z = 2 * pl.program_id(0) + chip
        device = 2 * meta_ref[2 + z] + dc
        s = 2 * z + ((meta_ref[0] + dc) & 1)
        ctx = (s >> 1) * 16 + m * 2 + (s & 1)
        for group in range(2):
            lens = [len_ref[use_row(rows_ref, ctx, 2 * group + n)] for n in range(2)]
            mask = slot < jnp.where(place < BTOK, lens[0], lens[1])
            rows = slice(group * GROUP, (group + 1) * GROUP)
            at = (2 * chip + (s & 1)) * USES + 2 * group
            keys, values = (
                jnp.concatenate([kv_ref[:, at + n, w].reshape(BTOK, HD) for n in range(2)], 0)
                for w in range(2)
            )
            query, grad = qg_ref[device, 0, rows, :], qg_ref[device, 1, rows, :]
            work.append((device, group, rows, at, ctx, mask, query, grad, keys, values))
    scored = [dot(query, keys, nt) for *_, query, _, keys, _ in work]
    dprobs = [dot(grad, values, nt) for *_, grad, _, values in work]
    soft = []
    for item, scores, dprob in zip(work, scored, dprobs):
        group, ctx, mask = item[1], item[4], item[5]
        scores = jnp.where(mask, scores * scaling, F32(-1e30))
        weights = jnp.exp(scores - jnp.max(scores, -1, keepdims=True))
        probs = weights * (1.0 / jnp.sum(weights, -1, keepdims=True))
        if group == 0:
            probs = jnp.where((row_at == 0) | (ctx > 0), probs, F32(0))
        delta = jnp.sum(probs * dprob, -1, keepdims=True)
        soft.append((probs.astype(BF), (probs * (dprob - delta) * scaling).astype(BF)))
    for (device, _, rows, _, _, _, _, _, keys, values), (probs_b, dscore) in zip(work, soft):
        out_ref[device, 0, rows, :] = dot(probs_b, values, nn).astype(BF)
        out_ref[device, 1, rows, :] = dot(dscore, keys, nn).astype(BF)
    for (_, _, _, at, _, _, query, grad, _, _), (probs_b, dscore) in zip(work, soft):
        grad_key = dot(dscore, query, tn).astype(BF)
        grad_value = dot(probs_b, grad, tn).astype(BF)
        for n in range(2):
            part = slice(n * BTOK, (n + 1) * BTOK)
            grad_ref[:, at + n, 0] = grad_key[part].reshape(PLANE, LINE, HD)
            grad_ref[:, at + n, 1] = grad_value[part].reshape(PLANE, LINE, HD)


def gather_grads(rows_ref, x_ref, out_ref, *sum_refs):
    m = pl.program_id(0)

    @pl.when(m == 0)
    def _():
        for ref in sum_refs:
            ref[...] = jnp.zeros_like(ref)

    for near in range(2):

        @pl.loop(0, LINE, unroll=4)
        def _(s):
            ctx = (s >> 1) * 16 + (2 * m + near) * 2 + (s & 1)
            for u in range(USES):
                row = use_row(rows_ref, ctx, u)
                at = pl.ds(pl.multiple_of(row * 8, 8), 8)
                for n in range(2):
                    wide = x_ref[near, s * USES + u, n].astype(F32)
                    for half in range(2):
                        sum_refs[2 * n + half][at, :] += wide[8 * half : 8 * half + 8]

    @pl.when(m == PLANE // 2 - 1)
    def _():
        for s in range(LINE):
            for n in range(2):
                part = sum_refs[2 * n + s // 8][pl.ds(s % 8, POOL, stride=8), :]
                out_ref[s, n] = part.astype(BF)


def spread(x_ref, out_ref):
    for head in range(LINE):
        for n in range(2):
            part = x_ref[head, n].astype(F32)
            out_ref[pl.ds(2 * head + n, part.shape[0], stride=2 * LINE), :] = part


VMEM = pl.BlockSpec(memory_space=pltpu.VMEM)
SMEM = pl.BlockSpec(memory_space=pltpu.SMEM)
LIMIT = pltpu.CompilerParams(vmem_limit_bytes=40 << 20)
LARGE = pltpu.CompilerParams(vmem_limit_bytes=60 << 20)


def shape(*dims, dtype=BF):
    return jax.ShapeDtypeStruct(dims, dtype)


def per_device(query, cotangent, pool, block_slot, block_length, neighbour_ids):
    columns = query.shape[1]
    rows = query.shape[0]
    me = lax.axis_index("ctx")
    z, core = me // 16, me % 2
    places = jnp.array([STEPS.index(dz) for dz in range(8)], jnp.int32)
    order = places[(z - jnp.arange(8, dtype=jnp.int32)) & 7]
    meta = jnp.concatenate([jnp.stack([z * 2 + core, (me // 2) % 8]).astype(jnp.int32), order])

    sent = pool.reshape(POOL, 2, LINE, HD).transpose(2, 0, 1, 3).reshape(LINE, 2 * POOL, HD)
    line_kv = exchange(sent, LINES)

    own = lax.dynamic_update_slice(
        jnp.zeros((CTX * USES,), jnp.int32), block_slot[neighbour_ids.reshape(-1)], (me * USES,)
    )
    pool_rows = lax.psum(own, "ctx")

    before = ring_move(jnp.stack([query[rows - 1], cotangent[rows - 1]]), 1)
    pool_rows, before = lax.optimization_barrier((pool_rows, before))
    other = pl.pallas_call(
        split_other,
        out_shape=shape(8, 2, rows, HD),
        in_specs=[VMEM, VMEM, VMEM, SMEM],
        out_specs=VMEM,
        compiler_params=LIMIT,
    )(query, cotangent, before, meta)
    other = line_move(other, 0, 1)

    plane_spec = pl.BlockSpec((2, LINE * USES, 2, LINE, HD), lambda i, *_: (i, 0, 0, 0, 0))
    line_spec = pl.BlockSpec((LINE, 2, POOL, HD), lambda i, *_: (0, 0, 0, 0))
    picked = pl.pallas_call(
        pick,
        out_shape=shape(PLANE, LINE * USES, 2, LINE, HD),
        grid_spec=pltpu.PrefetchScalarGridSpec(
            num_scalar_prefetch=1,
            grid=(PLANE // 2,),
            in_specs=[pl.BlockSpec((LINE, 2 * POOL, HD), lambda i, *_: (0, 0, 0))],
            out_specs=plane_spec,
            scratch_shapes=[
                pltpu.VMEM((2 * LINE * POOL, HD), F32),
                pltpu.VMEM((POOL, 2, LINE, HD), BF),
            ],
        ),
        compiler_params=LARGE,
        cost_estimate=pl.CostEstimate(flops=0, transcendentals=0, bytes_accessed=24 << 20),
    )(pool_rows, line_kv)
    picked, other = lax.optimization_barrier((picked, other))
    fetched = exchange(picked, PLANES)
    split = pl.pallas_call(
        split_own,
        out_shape=[shape(2, 2, rows, HD)] * 8,
        in_specs=[VMEM, VMEM, VMEM, SMEM, VMEM],
        out_specs=[VMEM] * 8,
        compiler_params=LIMIT,
    )(query, cotangent, before, meta, other)

    head_rows = jnp.concatenate(
        [split[0]] + [line_move(split[k], STEPS[k], 0) for k in range(1, 8)]
    )

    rows_spec = pl.BlockSpec((LINE, 2, rows, HD), lambda i, *_: (0, 0, 0, 0))
    uses_spec = pl.BlockSpec((PLANE, 4 * USES, 2, LINE, HD), lambda i, *_: (0, i, 0, 0, 0))
    results, grads = pl.pallas_call(
        attend,
        out_shape=(shape(LINE, 2, rows, HD), shape(PLANE, LINE * USES, 2, LINE, HD)),
        grid_spec=pltpu.PrefetchScalarGridSpec(
            num_scalar_prefetch=3,
            grid=(LINE // 4,),
            in_specs=[rows_spec, uses_spec],
            out_specs=(rows_spec, uses_spec),
        ),
        compiler_params=LARGE,
    )(pool_rows, block_length, meta, head_rows, fetched)

    returned = exchange(grads, PLANES)

    results = results.reshape(8, 2, 2, rows, HD)
    back = [results[0]] + [line_move(results[k], -STEPS[k], 0) for k in range(1, 8)]
    att_part, dq_part, edge_out = pl.pallas_call(
        join_rows,
        out_shape=(shape(rows, columns), shape(rows, columns), shape(2, columns)),
        in_specs=[VMEM] * 9 + [SMEM],
        out_specs=(VMEM, VMEM, VMEM),
        compiler_params=LIMIT,
    )(*back, line_move(jnp.stack([part[1] for part in back]), 0, 1), meta)
    returned, edge_out = lax.optimization_barrier((returned, edge_out))
    summed = pl.pallas_call(
        gather_grads,
        out_shape=shape(LINE, 2, POOL, HD),
        grid_spec=pltpu.PrefetchScalarGridSpec(
            num_scalar_prefetch=1,
            grid=(PLANE // 2,),
            in_specs=[plane_spec],
            out_specs=line_spec,
            scratch_shapes=[pltpu.VMEM((POOL * 8, HD), F32)] * 4,
        ),
        compiler_params=LIMIT,
    )(pool_rows, returned)
    after = ring_move(edge_out, -1)
    attended, d_query = pl.pallas_call(
        close_rows,
        out_shape=(shape(rows, columns), shape(rows, columns)),
        in_specs=[VMEM, VMEM, VMEM],
        out_specs=(VMEM, VMEM),
        compiler_params=LIMIT,
    )(att_part, dq_part, after)

    own_grads = exchange(summed, LINES)
    chunk = 64
    wide = pl.pallas_call(
        spread,
        out_shape=shape(POOL * 2 * LINE, HD, dtype=F32),
        grid=(POOL // chunk,),
        in_specs=[pl.BlockSpec((LINE, 2, chunk, HD), lambda i: (0, 0, i, 0))],
        out_specs=pl.BlockSpec((chunk * 2 * LINE, HD), lambda i: (i, 0)),
        compiler_params=LIMIT,
    )(own_grads)
    d_pool = wide.reshape(POOL, LINE, 2, HD).transpose(0, 2, 1, 3).reshape(pool.shape)
    return (attended, d_query, d_pool)


def solution(mesh):
    placed = (
        P("ctx", "head"),
        P("ctx", "head"),
        P(None, "ctx", None, "head"),
        P(),
        P(),
        P("ctx", None),
    )
    return jax.shard_map(
        per_device,
        mesh=mesh,
        in_specs=placed,
        out_specs=(P("ctx", "head"), P("ctx", "head"), P(None, "ctx", None, "head")),
        check_vma=False,
    )
```

```python
import functools
import math

import jax
import jax.numpy as jnp
from jax import lax
from jax.experimental import pallas as pl
from jax.experimental.pallas import tpu as pltpu
from jax.sharding import PartitionSpec as P

HD = 128
GROUP = 64
BTOK = 128
POOL = 256
CTX = 128
LINE = 16
PLANE = 8
USES = 4
BF = jnp.bfloat16
F32 = jnp.float32


def ctx_of(s, m):
    return (s // 2) * 16 + m * 2 + s % 2


LINES = [[ctx_of(s, m) for s in range(LINE)] for m in range(PLANE)]
PLANES = [[ctx_of(s, m) for m in range(PLANE)] for s in range(LINE)]
STEPS = (0, 4, 3, 5, 2, 6, 1, 7)


def line_move(value, dz, dc):
    pairs = [
        (ctx_of(s, m), ctx_of((s // 2 + dz) % 8 * 2 + (s % 2 + dc) % 2, m))
        for s in range(LINE)
        for m in range(PLANE)
    ]
    return lax.ppermute(value, "ctx", pairs)


def ring_move(value, step):
    return lax.ppermute(value, "ctx", [(i, (i + step) % CTX) for i in range(CTX)])


def exchange(value, groups):
    return lax.all_to_all(
        value, "ctx", split_axis=0, concat_axis=0, tiled=True, axis_index_groups=groups
    )


def use_row(rows_ref, ctx, u):
    return rows_ref[(ctx * USES + u - 2) & (2 * POOL - 1)]


def head_columns(meta_ref, dz, dc):
    head = ((meta_ref[0] >> 1) + dz & 7) * 2 + (meta_ref[0] + dc & 1)
    return pl.ds(pl.multiple_of(head * HD, HD), HD)


def late_rows(wide, first):
    at = lax.broadcasted_iota(jnp.int32, (2 * GROUP, HD), 0)
    return jnp.where(at == 0, first.astype(F32), pltpu.roll(wide.astype(F32), 1, 0)).astype(BF)


def split_other(q_ref, g_ref, meta_ref, out_ref):
    for k, dz in enumerate(STEPS):
        cols = head_columns(meta_ref, dz, 1)
        for n, ref in enumerate((q_ref, g_ref)):
            out_ref[k, n] = ref[:, cols]


def split_own(q_ref, g_ref, prev_ref, prev_other_ref, meta_ref, other_ref, *out_refs):
    for k, dz in enumerate(STEPS):
        cols = head_columns(meta_ref, dz, 0)
        for n, ref in enumerate((q_ref, g_ref)):
            row = slice(n, n + 1)
            out_refs[k][0, n] = late_rows(ref[:, cols], prev_ref[row, cols])
            out_refs[k][1, n] = late_rows(other_ref[k, n], prev_other_ref[row, cols])


def join_rows(*refs):
    own_refs, (other_ref, meta_ref, att_ref, dq_ref, edge_ref) = refs[:8], refs[8:]
    for k, dz in enumerate(STEPS):
        for dc in range(2):
            cols = head_columns(meta_ref, dz, dc)
            for n, ref in enumerate((att_ref, dq_ref)):
                wide = (other_ref[k, n] if dc else own_refs[k][0, n]).astype(F32)
                ref[:, cols] = pltpu.roll(wide, 2 * GROUP - 1, 0).astype(BF)
                edge_ref[n : n + 1, cols] = wide[0:1].astype(BF)


def close_rows(att_in, dq_in, edge_ref, att_ref, dq_ref):
    rows = lax.broadcasted_iota(jnp.int32, att_in.shape, 0)
    last = rows == 2 * GROUP - 1
    for n, (ref, out) in enumerate(((att_in, att_ref), (dq_in, dq_ref))):
        edge = edge_ref[n : n + 1, :].astype(F32)
        out[...] = jnp.where(last, edge, ref[...].astype(F32)).astype(BF)


def pick(rows_ref, x_ref, out_ref, wide_ref, block_ref):
    m = pl.program_id(0)

    @pl.when(m == 0)
    def _():
        for s in range(LINE):
            wide_ref[pl.ds(s, 2 * POOL, stride=LINE), :] = x_ref[s].astype(F32)

        @pl.loop(0, POOL // 8)
        def _(i):
            at = pl.ds(pl.multiple_of(i * 256, 256), 256)
            block_ref[pl.ds(i * 8, 8)] = wide_ref[at, :].astype(BF).reshape(8, 2, LINE, HD)

    for near in range(2):

        @pl.loop(0, LINE, unroll=4)
        def _(s):
            ctx = (s >> 1) * 16 + (2 * m + near) * 2 + (s & 1)
            for u in range(USES):
                out_ref[near, s * USES + u] = block_ref[use_row(rows_ref, ctx, u)]


def attend(rows_ref, len_ref, meta_ref, qg_ref, kv_ref, out_ref, grad_ref):
    scaling = 1.0 / math.sqrt(HD)
    m = meta_ref[1]
    place = lax.broadcasted_iota(jnp.int32, (1, 2 * BTOK), 1)
    within = place % BTOK
    slot = ((within % LINE) // 2) * 16 + (within // LINE) * 2 + within % 2
    row_at = lax.broadcasted_iota(jnp.int32, (GROUP, 1), 0)
    nn, nt, tn = (((((i,), (j,)), ((), ()))) for i, j in ((1, 0), (1, 1), (0, 0)))
    dot = functools.partial(lax.dot_general, preferred_element_type=F32)
    work = []
    for chip, dc in ((0, 0), (0, 1), (1, 0), (1, 1)):
        z = 2 * pl.program_id(0) + chip
        device = 2 * meta_ref[2 + z] + dc
        s = 2 * z + ((meta_ref[0] + dc) & 1)
        ctx = (s >> 1) * 16 + m * 2 + (s & 1)
        for group in range(2):
            lens = [len_ref[use_row(rows_ref, ctx, 2 * group + n)] for n in range(2)]
            mask = slot < jnp.where(place < BTOK, lens[0], lens[1])
            rows = slice(group * GROUP, (group + 1) * GROUP)
            at = (2 * chip + (s & 1)) * USES + 2 * group
            keys, values = (
                jnp.concatenate([kv_ref[:, at + n, w].reshape(BTOK, HD) for n in range(2)], 0)
                for w in range(2)
            )
            query, grad = qg_ref[device, 0, rows, :], qg_ref[device, 1, rows, :]
            work.append((device, group, rows, at, ctx, mask, query, grad, keys, values))
    scored = [dot(query, keys, nt) for *_, query, _, keys, _ in work]
    dprobs = [dot(grad, values, nt) for *_, grad, _, values in work]
    soft = []
    for item, scores, dprob in zip(work, scored, dprobs):
        group, ctx, mask = item[1], item[4], item[5]
        scores = jnp.where(mask, scores * scaling, F32(-1e30))
        weights = jnp.exp(scores - jnp.max(scores, -1, keepdims=True))
        probs = weights * (1.0 / jnp.sum(weights, -1, keepdims=True))
        if group == 0:
            probs = jnp.where((row_at == 0) | (ctx > 0), probs, F32(0))
        delta = jnp.sum(probs * dprob, -1, keepdims=True)
        soft.append((probs.astype(BF), (probs * (dprob - delta) * scaling).astype(BF)))
    for (device, _, rows, _, _, _, _, _, keys, values), (probs_b, dscore) in zip(work, soft):
        out_ref[device, 0, rows, :] = dot(probs_b, values, nn).astype(BF)
        out_ref[device, 1, rows, :] = dot(dscore, keys, nn).astype(BF)
    for (_, _, _, at, _, _, query, grad, _, _), (probs_b, dscore) in zip(work, soft):
        grad_key = dot(dscore, query, tn).astype(BF)
        grad_value = dot(probs_b, grad, tn).astype(BF)
        for n in range(2):
            part = slice(n * BTOK, (n + 1) * BTOK)
            grad_ref[:, at + n, 0] = grad_key[part].reshape(PLANE, LINE, HD)
            grad_ref[:, at + n, 1] = grad_value[part].reshape(PLANE, LINE, HD)


def gather_grads(rows_ref, x_ref, out_ref, *sum_refs):
    m = pl.program_id(0)

    @pl.when(m == 0)
    def _():
        for ref in sum_refs:
            ref[...] = jnp.zeros_like(ref)

    for near in range(2):

        @pl.loop(0, LINE, unroll=4)
        def _(s):
            ctx = (s >> 1) * 16 + (2 * m + near) * 2 + (s & 1)
            for u in range(USES):
                row = use_row(rows_ref, ctx, u)
                at = pl.ds(pl.multiple_of(row * 8, 8), 8)
                for n in range(2):
                    wide = x_ref[near, s * USES + u, n].astype(F32)
                    for half in range(2):
                        sum_refs[2 * n + half][at, :] += wide[8 * half : 8 * half + 8]

    @pl.when(m == PLANE // 2 - 1)
    def _():
        for s in range(LINE):
            for n in range(2):
                part = sum_refs[2 * n + s // 8][pl.ds(s % 8, POOL, stride=8), :]
                out_ref[s, n] = part.astype(BF)


def spread(x_ref, out_ref):
    for head in range(LINE):
        for n in range(2):
            part = x_ref[head, n].astype(F32)
            out_ref[pl.ds(2 * head + n, part.shape[0], stride=2 * LINE), :] = part


VMEM = pl.BlockSpec(memory_space=pltpu.VMEM)
SMEM = pl.BlockSpec(memory_space=pltpu.SMEM)
LIMIT = pltpu.CompilerParams(vmem_limit_bytes=24 << 20)


def shape(*dims, dtype=BF):
    return jax.ShapeDtypeStruct(dims, dtype)


def per_device(query, cotangent, pool, block_slot, block_length, neighbour_ids):
    columns = query.shape[1]
    rows = query.shape[0]
    me = lax.axis_index("ctx")
    z, core = me // 16, me % 2
    places = jnp.array([STEPS.index(dz) for dz in range(8)], jnp.int32)
    order = places[(z - jnp.arange(8, dtype=jnp.int32)) & 7]
    meta = jnp.concatenate([jnp.stack([z * 2 + core, (me // 2) % 8]).astype(jnp.int32), order])

    sent = pool.reshape(POOL, 2, LINE, HD).transpose(2, 0, 1, 3).reshape(LINE, 2 * POOL, HD)
    line_kv = exchange(sent, LINES)

    own = lax.dynamic_update_slice(
        jnp.zeros((CTX * USES,), jnp.int32), block_slot[neighbour_ids.reshape(-1)], (me * USES,)
    )

    other = pl.pallas_call(
        split_other,
        out_shape=shape(8, 2, rows, HD),
        in_specs=[VMEM, VMEM, SMEM],
        out_specs=VMEM,
        compiler_params=LIMIT,
    )(query, cotangent, meta)
    own, other = lax.optimization_barrier((own, other))
    pool_rows = lax.psum(own, "ctx")
    other = line_move(other, 0, 1)

    last = jnp.stack([query[rows - 1], cotangent[rows - 1]])
    before = ring_move(last, 1)
    before_other = lax.ppermute(last, "ctx", [(((i ^ 1) - 1) % CTX, i) for i in range(CTX)])
    pool_rows, before, before_other = lax.optimization_barrier((pool_rows, before, before_other))

    plane_spec = pl.BlockSpec((2, LINE * USES, 2, LINE, HD), lambda i, *_: (i, 0, 0, 0, 0))
    line_spec = pl.BlockSpec((LINE, 2, POOL, HD), lambda i, *_: (0, 0, 0, 0))
    picked = pl.pallas_call(
        pick,
        out_shape=shape(PLANE, LINE * USES, 2, LINE, HD),
        grid_spec=pltpu.PrefetchScalarGridSpec(
            num_scalar_prefetch=1,
            grid=(PLANE // 2,),
            in_specs=[pl.BlockSpec((LINE, 2 * POOL, HD), lambda i, *_: (0, 0, 0))],
            out_specs=plane_spec,
            scratch_shapes=[
                pltpu.VMEM((2 * LINE * POOL, HD), F32),
                pltpu.VMEM((POOL, 2, LINE, HD), BF),
            ],
        ),
        compiler_params=LIMIT,
        cost_estimate=pl.CostEstimate(flops=0, transcendentals=0, bytes_accessed=24 << 20),
    )(pool_rows, line_kv)
    picked, other = lax.optimization_barrier((picked, other))
    fetched = exchange(picked, PLANES)
    split = pl.pallas_call(
        split_own,
        out_shape=[shape(2, 2, rows, HD)] * 8,
        in_specs=[VMEM, VMEM, VMEM, VMEM, SMEM, VMEM],
        out_specs=[VMEM] * 8,
        compiler_params=LIMIT,
    )(query, cotangent, before, before_other, meta, other)

    head_rows = jnp.concatenate(
        [split[0]] + [line_move(split[k], STEPS[k], 0) for k in range(1, 8)]
    )

    rows_spec = pl.BlockSpec((LINE, 2, rows, HD), lambda i, *_: (0, 0, 0, 0))
    uses_spec = pl.BlockSpec((PLANE, 4 * USES, 2, LINE, HD), lambda i, *_: (0, i, 0, 0, 0))
    results, grads = pl.pallas_call(
        attend,
        out_shape=(shape(LINE, 2, rows, HD), shape(PLANE, LINE * USES, 2, LINE, HD)),
        grid_spec=pltpu.PrefetchScalarGridSpec(
            num_scalar_prefetch=3,
            grid=(LINE // 4,),
            in_specs=[rows_spec, uses_spec],
            out_specs=(rows_spec, uses_spec),
        ),
        compiler_params=LIMIT,
    )(pool_rows, block_length, meta, head_rows, fetched)

    returned = exchange(grads, PLANES)

    results = results.reshape(8, 2, 2, rows, HD)
    back = [results[0]] + [line_move(results[k], -STEPS[k], 0) for k in range(1, 8)]
    att_part, dq_part, edge_out = pl.pallas_call(
        join_rows,
        out_shape=(shape(rows, columns), shape(rows, columns), shape(2, columns)),
        in_specs=[VMEM] * 9 + [SMEM],
        out_specs=(VMEM, VMEM, VMEM),
        compiler_params=LIMIT,
    )(*back, line_move(jnp.stack([part[1] for part in back]), 0, 1), meta)
    returned, edge_out = lax.optimization_barrier((returned, edge_out))
    summed = pl.pallas_call(
        gather_grads,
        out_shape=shape(LINE, 2, POOL, HD),
        grid_spec=pltpu.PrefetchScalarGridSpec(
            num_scalar_prefetch=1,
            grid=(PLANE // 2,),
            in_specs=[plane_spec],
            out_specs=line_spec,
            scratch_shapes=[pltpu.VMEM((POOL * 8, HD), F32)] * 4,
        ),
        compiler_params=LIMIT,
    )(pool_rows, returned)
    after = ring_move(edge_out, -1)
    attended, d_query = pl.pallas_call(
        close_rows,
        out_shape=(shape(rows, columns), shape(rows, columns)),
        in_specs=[VMEM, VMEM, VMEM],
        out_specs=(VMEM, VMEM),
        compiler_params=LIMIT,
    )(att_part, dq_part, after)

    own_grads = exchange(summed, LINES)
    chunk = 64
    wide = pl.pallas_call(
        spread,
        out_shape=shape(POOL * 2 * LINE, HD, dtype=F32),
        grid=(POOL // chunk,),
        in_specs=[pl.BlockSpec((LINE, 2, chunk, HD), lambda i: (0, 0, i, 0))],
        out_specs=pl.BlockSpec((chunk * 2 * LINE, HD), lambda i: (i, 0)),
        compiler_params=LIMIT,
    )(own_grads)
    d_pool = wide.reshape(POOL, LINE, 2, HD).transpose(0, 2, 1, 3).reshape(pool.shape)
    return (attended, d_query, d_pool)


def solution(mesh):
    placed = (
        P("ctx", "head"),
        P("ctx", "head"),
        P(None, "ctx", None, "head"),
        P(),
        P(),
        P("ctx", None),
    )
    return jax.shard_map(
        per_device,
        mesh=mesh,
        in_specs=placed,
        out_specs=(P("ctx", "head"), P("ctx", "head"), P(None, "ctx", None, "head")),
        check_vma=False,
    )
```

```python
import functools
import math

import jax
import jax.numpy as jnp
from jax import lax
from jax.experimental import pallas as pl
from jax.experimental.pallas import tpu as pltpu
from jax.sharding import PartitionSpec as P

HD = 128
GROUP = 64
BTOK = 128
POOL = 256
CTX = 128
LINE = 16
PLANE = 8
USES = 4
BF = jnp.bfloat16
F32 = jnp.float32


def ctx_of(s, m):
    return (s // 2) * 16 + m * 2 + s % 2


LINES = [[ctx_of(s, m) for s in range(LINE)] for m in range(PLANE)]
PLANES = [[ctx_of(s, m) for m in range(PLANE)] for s in range(LINE)]
STEPS = (0, 4, 3, 5, 2, 6, 1, 7)


def line_move(value, dz, dc):
    pairs = [
        (ctx_of(s, m), ctx_of((s // 2 + dz) % 8 * 2 + (s % 2 + dc) % 2, m))
        for s in range(LINE)
        for m in range(PLANE)
    ]
    return lax.ppermute(value, "ctx", pairs)


def ring_move(value, step):
    return lax.ppermute(value, "ctx", [(i, (i + step) % CTX) for i in range(CTX)])


def exchange(value, groups):
    return lax.all_to_all(
        value, "ctx", split_axis=0, concat_axis=0, tiled=True, axis_index_groups=groups
    )


def use_row(rows_ref, ctx, u):
    return rows_ref[(ctx * USES + u - 2) & (2 * POOL - 1)]


def head_columns(meta_ref, dz, dc):
    head = ((meta_ref[0] >> 1) + dz & 7) * 2 + (meta_ref[0] + dc & 1)
    return pl.ds(pl.multiple_of(head * HD, HD), HD)


def late_rows(wide, first):
    at = lax.broadcasted_iota(jnp.int32, (2 * GROUP, HD), 0)
    return jnp.where(at == 0, first.astype(F32), pltpu.roll(wide.astype(F32), 1, 0)).astype(BF)


def split_other(q_ref, g_ref, meta_ref, out_ref):
    for k, dz in enumerate(STEPS):
        cols = head_columns(meta_ref, dz, 1)
        for n, ref in enumerate((q_ref, g_ref)):
            out_ref[k, n] = ref[:, cols]


def split_own(q_ref, g_ref, prev_ref, prev_other_ref, meta_ref, other_ref, *out_refs):
    for k, dz in enumerate(STEPS):
        cols = head_columns(meta_ref, dz, 0)
        for n, ref in enumerate((q_ref, g_ref)):
            row = slice(n, n + 1)
            out_refs[k][0, n] = late_rows(ref[:, cols], prev_ref[row, cols])
            out_refs[k][1, n] = late_rows(other_ref[k, n], prev_other_ref[row, cols])


def join_rows(*refs):
    own_refs, (other_ref, meta_ref, att_ref, dq_ref, edge_ref) = refs[:8], refs[8:]
    for k, dz in enumerate(STEPS):
        for dc in range(2):
            cols = head_columns(meta_ref, dz, dc)
            for n, ref in enumerate((att_ref, dq_ref)):
                wide = (other_ref[k, n] if dc else own_refs[k][0, n]).astype(F32)
                ref[:, cols] = pltpu.roll(wide, 2 * GROUP - 1, 0).astype(BF)
                edge_ref[n : n + 1, cols] = wide[0:1].astype(BF)


def close_rows(att_in, dq_in, edge_ref, att_ref, dq_ref):
    rows = lax.broadcasted_iota(jnp.int32, att_in.shape, 0)
    last = rows == 2 * GROUP - 1
    for n, (ref, out) in enumerate(((att_in, att_ref), (dq_in, dq_ref))):
        edge = edge_ref[n : n + 1, :].astype(F32)
        out[...] = jnp.where(last, edge, ref[...].astype(F32)).astype(BF)


def pick(rows_ref, x_ref, out_ref, wide_ref, block_ref):
    m = pl.program_id(0)

    @pl.when(m == 0)
    def _():
        for s in range(LINE):
            wide_ref[pl.ds(s, 2 * POOL, stride=LINE), :] = x_ref[s].astype(F32)

        @pl.loop(0, POOL // 8)
        def _(i):
            at = pl.ds(pl.multiple_of(i * 256, 256), 256)
            block_ref[pl.ds(i * 8, 8)] = wide_ref[at, :].astype(BF).reshape(8, 2, LINE, HD)

    for near in range(4):

        @pl.loop(0, LINE, unroll=4)
        def _(s):
            ctx = (s >> 1) * 16 + (4 * m + near) * 2 + (s & 1)
            for u in range(USES):
                out_ref[near, s * USES + u] = block_ref[use_row(rows_ref, ctx, u)]


def attend(rows_ref, len_ref, meta_ref, qg_ref, kv_ref, out_ref, grad_ref):
    scaling = 1.0 / math.sqrt(HD)
    m = meta_ref[1]
    place = lax.broadcasted_iota(jnp.int32, (1, 2 * BTOK), 1)
    within = place % BTOK
    slot = ((within % LINE) // 2) * 16 + (within // LINE) * 2 + within % 2
    row_at = lax.broadcasted_iota(jnp.int32, (GROUP, 1), 0)
    nn, nt, tn = (((((i,), (j,)), ((), ()))) for i, j in ((1, 0), (1, 1), (0, 0)))
    dot = functools.partial(lax.dot_general, preferred_element_type=F32)
    work = []
    for chip, dc in ((0, 0), (0, 1), (1, 0), (1, 1)):
        z = 2 * pl.program_id(0) + chip
        device = 2 * meta_ref[2 + z] + dc
        s = 2 * z + ((meta_ref[0] + dc) & 1)
        ctx = (s >> 1) * 16 + m * 2 + (s & 1)
        for group in range(2):
            lens = [len_ref[use_row(rows_ref, ctx, 2 * group + n)] for n in range(2)]
            mask = slot < jnp.where(place < BTOK, lens[0], lens[1])
            rows = slice(group * GROUP, (group + 1) * GROUP)
            at = (2 * chip + (s & 1)) * USES + 2 * group
            keys, values = (
                jnp.concatenate([kv_ref[:, at + n, w].reshape(BTOK, HD) for n in range(2)], 0)
                for w in range(2)
            )
            query, grad = qg_ref[device, 0, rows, :], qg_ref[device, 1, rows, :]
            work.append((device, group, rows, at, ctx, mask, query, grad, keys, values))
    scored = [dot(query, keys, nt) for *_, query, _, keys, _ in work]
    dprobs = [dot(grad, values, nt) for *_, grad, _, values in work]
    soft = []
    for item, scores, dprob in zip(work, scored, dprobs):
        group, ctx, mask = item[1], item[4], item[5]
        scores = jnp.where(mask, scores * scaling, F32(-1e30))
        weights = jnp.exp(scores - jnp.max(scores, -1, keepdims=True))
        probs = weights * (1.0 / jnp.sum(weights, -1, keepdims=True))
        if group == 0:
            probs = jnp.where((row_at == 0) | (ctx > 0), probs, F32(0))
        delta = jnp.sum(probs * dprob, -1, keepdims=True)
        soft.append((probs.astype(BF), (probs * (dprob - delta) * scaling).astype(BF)))
    for (device, _, rows, _, _, _, _, _, keys, values), (probs_b, dscore) in zip(work, soft):
        out_ref[device, 0, rows, :] = dot(probs_b, values, nn).astype(BF)
        out_ref[device, 1, rows, :] = dot(dscore, keys, nn).astype(BF)
    for (_, _, _, at, _, _, query, grad, _, _), (probs_b, dscore) in zip(work, soft):
        grad_key = dot(dscore, query, tn).astype(BF)
        grad_value = dot(probs_b, grad, tn).astype(BF)
        for n in range(2):
            part = slice(n * BTOK, (n + 1) * BTOK)
            grad_ref[:, at + n, 0] = grad_key[part].reshape(PLANE, LINE, HD)
            grad_ref[:, at + n, 1] = grad_value[part].reshape(PLANE, LINE, HD)


def gather_grads(rows_ref, x_ref, out_ref, *sum_refs):
    m = pl.program_id(0)

    @pl.when(m == 0)
    def _():
        for ref in sum_refs:
            ref[...] = jnp.zeros_like(ref)

    for near in range(4):

        @pl.loop(0, LINE, unroll=4)
        def _(s):
            ctx = (s >> 1) * 16 + (4 * m + near) * 2 + (s & 1)
            for u in range(USES):
                row = use_row(rows_ref, ctx, u)
                at = pl.ds(pl.multiple_of(row * 8, 8), 8)
                for n in range(2):
                    wide = x_ref[near, s * USES + u, n].astype(F32)
                    for half in range(2):
                        sum_refs[2 * n + half][at, :] += wide[8 * half : 8 * half + 8]

    @pl.when(m == PLANE // 4 - 1)
    def _():
        for s in range(LINE):
            for n in range(2):
                part = sum_refs[2 * n + s // 8][pl.ds(s % 8, POOL, stride=8), :]
                out_ref[s, n] = part.astype(BF)


def spread(x_ref, out_ref):
    for head in range(LINE):
        for n in range(2):
            part = x_ref[head, n].astype(F32)
            out_ref[pl.ds(2 * head + n, part.shape[0], stride=2 * LINE), :] = part


VMEM = pl.BlockSpec(memory_space=pltpu.VMEM)
SMEM = pl.BlockSpec(memory_space=pltpu.SMEM)
LIMIT = pltpu.CompilerParams(vmem_limit_bytes=24 << 20)


def shape(*dims, dtype=BF):
    return jax.ShapeDtypeStruct(dims, dtype)


def per_device(query, cotangent, pool, block_slot, block_length, neighbour_ids):
    columns = query.shape[1]
    rows = query.shape[0]
    me = lax.axis_index("ctx")
    z, core = me // 16, me % 2
    places = jnp.array([STEPS.index(dz) for dz in range(8)], jnp.int32)
    order = places[(z - jnp.arange(8, dtype=jnp.int32)) & 7]
    meta = jnp.concatenate([jnp.stack([z * 2 + core, (me // 2) % 8]).astype(jnp.int32), order])

    sent = pool.reshape(POOL, 2, LINE, HD).transpose(2, 0, 1, 3).reshape(LINE, 2 * POOL, HD)
    line_kv = exchange(sent, LINES)

    own = lax.dynamic_update_slice(
        jnp.zeros((CTX * USES,), jnp.int32), block_slot[neighbour_ids.reshape(-1)], (me * USES,)
    )

    other = pl.pallas_call(
        split_other,
        out_shape=shape(8, 2, rows, HD),
        in_specs=[VMEM, VMEM, SMEM],
        out_specs=VMEM,
        compiler_params=LIMIT,
    )(query, cotangent, meta)
    own, other = lax.optimization_barrier((own, other))
    pool_rows = lax.psum(own, "ctx")
    other = line_move(other, 0, 1)

    last = jnp.stack([query[rows - 1], cotangent[rows - 1]])
    before = ring_move(last, 1)
    before_other = lax.ppermute(last, "ctx", [(((i ^ 1) - 1) % CTX, i) for i in range(CTX)])
    pool_rows, before, before_other = lax.optimization_barrier((pool_rows, before, before_other))

    plane_spec = pl.BlockSpec((4, LINE * USES, 2, LINE, HD), lambda i, *_: (i, 0, 0, 0, 0))
    line_spec = pl.BlockSpec((LINE, 2, POOL, HD), lambda i, *_: (0, 0, 0, 0))
    picked = pl.pallas_call(
        pick,
        out_shape=shape(PLANE, LINE * USES, 2, LINE, HD),
        grid_spec=pltpu.PrefetchScalarGridSpec(
            num_scalar_prefetch=1,
            grid=(PLANE // 4,),
            in_specs=[pl.BlockSpec((LINE, 2 * POOL, HD), lambda i, *_: (0, 0, 0))],
            out_specs=plane_spec,
            scratch_shapes=[
                pltpu.VMEM((2 * LINE * POOL, HD), F32),
                pltpu.VMEM((POOL, 2, LINE, HD), BF),
            ],
        ),
        compiler_params=LIMIT,
        cost_estimate=pl.CostEstimate(flops=0, transcendentals=0, bytes_accessed=24 << 20),
    )(pool_rows, line_kv)
    picked, other = lax.optimization_barrier((picked, other))
    fetched = exchange(picked, PLANES)
    split = pl.pallas_call(
        split_own,
        out_shape=[shape(2, 2, rows, HD)] * 8,
        in_specs=[VMEM, VMEM, VMEM, VMEM, SMEM, VMEM],
        out_specs=[VMEM] * 8,
        compiler_params=LIMIT,
    )(query, cotangent, before, before_other, meta, other)

    head_rows = jnp.concatenate(
        [split[0]] + [line_move(split[k], STEPS[k], 0) for k in range(1, 8)]
    )

    rows_spec = pl.BlockSpec((LINE, 2, rows, HD), lambda i, *_: (0, 0, 0, 0))
    uses_spec = pl.BlockSpec((PLANE, 4 * USES, 2, LINE, HD), lambda i, *_: (0, i, 0, 0, 0))
    results, grads = pl.pallas_call(
        attend,
        out_shape=(shape(LINE, 2, rows, HD), shape(PLANE, LINE * USES, 2, LINE, HD)),
        grid_spec=pltpu.PrefetchScalarGridSpec(
            num_scalar_prefetch=3,
            grid=(LINE // 4,),
            in_specs=[rows_spec, uses_spec],
            out_specs=(rows_spec, uses_spec),
        ),
        compiler_params=LIMIT,
    )(pool_rows, block_length, meta, head_rows, fetched)

    returned = exchange(grads, PLANES)

    results = results.reshape(8, 2, 2, rows, HD)
    back = [results[0]] + [line_move(results[k], -STEPS[k], 0) for k in range(1, 8)]
    att_part, dq_part, edge_out = pl.pallas_call(
        join_rows,
        out_shape=(shape(rows, columns), shape(rows, columns), shape(2, columns)),
        in_specs=[VMEM] * 9 + [SMEM],
        out_specs=(VMEM, VMEM, VMEM),
        compiler_params=LIMIT,
    )(*back, line_move(jnp.stack([part[1] for part in back]), 0, 1), meta)
    returned, edge_out = lax.optimization_barrier((returned, edge_out))
    summed = pl.pallas_call(
        gather_grads,
        out_shape=shape(LINE, 2, POOL, HD),
        grid_spec=pltpu.PrefetchScalarGridSpec(
            num_scalar_prefetch=1,
            grid=(PLANE // 4,),
            in_specs=[plane_spec],
            out_specs=line_spec,
            scratch_shapes=[pltpu.VMEM((POOL * 8, HD), F32)] * 4,
        ),
        compiler_params=LIMIT,
    )(pool_rows, returned)
    after = ring_move(edge_out, -1)
    attended, d_query = pl.pallas_call(
        close_rows,
        out_shape=(shape(rows, columns), shape(rows, columns)),
        in_specs=[VMEM, VMEM, VMEM],
        out_specs=(VMEM, VMEM),
        compiler_params=LIMIT,
    )(att_part, dq_part, after)

    own_grads = exchange(summed, LINES)
    chunk = 64
    wide = pl.pallas_call(
        spread,
        out_shape=shape(POOL * 2 * LINE, HD, dtype=F32),
        grid=(POOL // chunk,),
        in_specs=[pl.BlockSpec((LINE, 2, chunk, HD), lambda i: (0, 0, i, 0))],
        out_specs=pl.BlockSpec((chunk * 2 * LINE, HD), lambda i: (i, 0)),
        compiler_params=LIMIT,
    )(own_grads)
    d_pool = wide.reshape(POOL, LINE, 2, HD).transpose(0, 2, 1, 3).reshape(pool.shape)
    return (attended, d_query, d_pool)


def solution(mesh):
    placed = (
        P("ctx", "head"),
        P("ctx", "head"),
        P(None, "ctx", None, "head"),
        P(),
        P(),
        P("ctx", None),
    )
    return jax.shard_map(
        per_device,
        mesh=mesh,
        in_specs=placed,
        out_specs=(P("ctx", "head"), P("ctx", "head"), P(None, "ctx", None, "head")),
        check_vma=False,
    )
```
